32 devices in a mesh: grp: 2 (over y), gx: 4 (over z), gy: 4 (over x, core).
Axes of the slice: x: 2, y: 2, z: 4, core: 2. Of those that a mesh axis runs over, the one named last changes fastest.
Arguments:
- samples: bfloat16 [2816, 65536], P('grp', ('gx', 'gy')), parts along dimension 0, may hold values from -400 to 400
- tile_owner: int32 [256], replicated, may hold values from 0 to 255, each once
Outputs:
- kernel_tiles: float32 [512, 4096], P(('grp', 'gx', 'gy')), parts along dimension 0
The draws below stay inside these ranges and needn't reach their ends.
There are 2 independent parts, one for each index of `grp`. The reference program is written for one: setup_inputs(seed, part) draws one part's arguments, and reference() takes and returns one part's arrays. A program takes and returns all parts, laid end to end along the dimension named above; an argument that names none is the same for every part. Nothing has to cross between parts.
Inputs may be any that keep to these rules, and one draw needn't show every extreme that they name: tile_owner holds each of 0 to 255 once; device k of the group (k = gx index * 4 + gy index) owns slots k * 16 to (k + 1) * 16 - 1; values of 253 and above mark empty slots.
All inputs are finite; a program needn't handle non-finite values.
Results may differ from the reference program's by a relative error of at most 0.0003.
Values sent between devices are 32-bit elements; how exact they have to be, the bound alone decides.
A program may use at most 64 MiB of HBM per device.

```python
import math
import jax
import jax.numpy as jnp
import numpy as np
from jax import lax

FEATURES = 65536
NS = 1408
TILE = 64
NT = 22
NLOW = 253
ALLSLOTS = 256


def draw_samples(key, part):
    key_rows = jax.random.fold_in(key, 11)
    key_cols = jax.random.fold_in(key, 12)
    key_base = jax.random.fold_in(key, 13)
    row_scale = jnp.exp(jax.random.uniform(key_rows, (NS, 1), jnp.float32) * math.log(10.0))
    ramp = jnp.exp(math.log(3.0) * jnp.arange(FEATURES, dtype=jnp.float32) / FEATURES)[None, :]
    col_scale = ramp * jnp.exp(jax.random.uniform(key_cols, (1, FEATURES), jnp.float32) * math.log(3.0))
    base = jnp.clip(jax.random.normal(key_base, (NS, FEATURES), jnp.float32), -4.0, 4.0)
    return (row_scale * col_scale * base).astype(jnp.bfloat16)


def setup_inputs(seed: int = 0, part: int = 0) -> dict:
    keys = jax.random.split(jax.random.key(seed), 3)
    part_keys = jax.random.split(jax.random.fold_in(keys[2], part), 3)
    return {
        "samples": draw_samples(jax.random.fold_in(jax.random.fold_in(keys[2], part), 71), part),
        "tile_owner": jax.random.permutation(keys[1], ALLSLOTS).astype(jnp.int32),
    }


def tile_coords(order):
    firsts = np.array([k * (k + 1) // 2 for k in range(1, NT)], dtype=np.int32)
    tile_row = lax.optimization_barrier(jnp.sum((order[:, None] >= jnp.asarray(firsts)[None, :]).astype(jnp.int32), axis=1)).astype(jnp.int32)
    tile_col = order - tile_row * (tile_row + 1) // 2
    is_live = order < NLOW
    tile_row = jnp.where(is_live, tile_row, 0).astype(jnp.int32)
    tile_col = jnp.where(is_live, tile_col, 0).astype(jnp.int32)
    return (tile_row, tile_col, is_live)

def reference(samples, tile_owner):
    gram = jnp.dot(samples, samples.T, preferred_element_type=jnp.float32)
    values = samples.astype(jnp.float32)
    meansq = lax.optimization_barrier(jnp.sum(values * values, axis=1)) / FEATURES + 1e-06
    inverse = 1.0 / jnp.sqrt(meansq)
    cosine = gram * inverse[:, None] * inverse[None, :] / jnp.sqrt(jnp.float32(FEATURES))
    blocked = cosine.reshape(NT, TILE, NT, TILE).transpose(0, 2, 1, 3)
    tile_row, tile_col, is_live = tile_coords(tile_owner)
    picked = blocked[tile_row, tile_col].reshape(tile_owner.shape[0], TILE * TILE)
    return picked * is_live[:, None].astype(jnp.float32)
```

```python
import functools

import jax
import jax.numpy as jnp
import numpy as np
from jax import lax
from jax.experimental import pallas as pl
from jax.experimental.pallas import tpu as pltpu
from jax.sharding import PartitionSpec as P

TILE = 64
HALF = TILE // 2
QUART = TILE // 4
ROWS = 256
MESH = pl.DeviceIdType.MESH


def tri(k):
    return k * (k + 1) // 2


def tables(slots_all, nt):
    dead = 8 * tri(nt // 2)
    table = np.zeros((6, slots_all), np.int32)
    table[0], table[1] = dead, dead
    t = 0
    for i in range(nt):
        for j in range(i + 1):
            first = 4 * (2 * (tri(i // 2) + j // 2) + i % 2)
            side = j % 2
            table[:, t] = (first + 2 * side, first + 2 * (1 - side), side, i, j // 2, side)
            t += 1
    assert t <= slots_all
    return table


def kernel(cfg, owner_ref, table_ref, x_ref, out_ref, a, g, h, buf, dg, inv, colb, scale, pk, flat,
           load_sem, pair_send, pair_recv, diag_send, diag_recv, ring_send, ring_recv):
    gx_n, gy_n, slots, nsub, features = cfg
    ring_n = gx_n * gy_n // 2
    sub = slots // nsub
    ns = a.shape[0]
    np_ = ns // 128
    gx, gy = lax.axis_index("gx"), lax.axis_index("gy")
    core = gy % 2
    row = gy // 2
    pos = row * gx_n + jnp.where(row % 2 == 0, gx, gx_n - 1 - gx)

    def coords_of(p):
        r = p // gx_n
        c = p % gx_n
        c = jnp.where(r % 2 == 0, c, gx_n - 1 - c)
        return c, r * 2 + core

    def device_of(p):
        c, y = coords_of(p)
        return {"gx": c, "gy": y}

    def first_slot(p):
        c, y = coords_of(p)
        return (c * gy_n + y) * slots

    partner = {"gx": gx, "gy": gy + 1 - 2 * core}

    starts = list(range(0, ns, ROWS))
    loads = []
    for n, r0 in enumerate(starts):
        size = min(ROWS, ns - r0)
        loads.append(pltpu.make_async_copy(x_ref.at[pl.ds(r0, size)], a.at[pl.ds(r0, size)], load_sem.at[n]))
        loads[-1].start()

    barrier = pltpu.get_barrier_semaphore()
    pl.semaphore_signal(barrier, inc=1, device_id=partner, device_id_type=MESH)

    @pl.loop(1, ring_n)
    def _(o):
        pl.semaphore_signal(barrier, inc=1, device_id=device_of((pos + o) % ring_n), device_id_type=MESH)

    dead = 8 * tri(np_)
    for n in range(4):
        g[dead + n] = jnp.zeros((QUART, 128), jnp.float32)
        h[dead + n] = jnp.zeros((QUART, 128), jnp.float32)

    def product(r0, size, c0, width):
        return lax.dot_general(
            a[pl.ds(r0, size), :], a[pl.ds(c0, width), :],
            (((1,), (1,)), ((), ())), preferred_element_type=jnp.float32,
        )

    def put(block, value):
        g[pl.ds(8 * block, 8)] = value.reshape(8, QUART, 128)

    pair_copies = []
    for n, r0 in enumerate(starts):
        size = min(ROWS, ns - r0)
        nq = size // 128
        loads[n].wait()

        if n:
            @pl.loop(0, n)
            def _(j):
                value = product(r0, size, pl.multiple_of(j * ROWS, ROWS), ROWS)
                for u in range(nq):
                    for v in range(2):
                        put(tri(r0 // 128 + u) + 2 * j + v, value[u * 128:(u + 1) * 128, v * 128:(v + 1) * 128])

        value = product(r0, size, r0, size)
        for u in range(nq):
            for v in range(u + 1):
                put(tri(r0 // 128 + u) + 2 * n + v, value[u * 128:(u + 1) * 128, v * 128:(v + 1) * 128])
        if n == 0:
            pl.semaphore_wait(barrier, ring_n)
        first, last = 8 * tri(r0 // 128), 8 * tri(r0 // 128 + nq)
        copy = pltpu.make_async_remote_copy(
            src_ref=g.at[pl.ds(first, last - first)], dst_ref=h.at[pl.ds(first, last - first)],
            send_sem=pair_send.at[n], recv_sem=pair_recv.at[n], device_id=partner, device_id_type=MESH)
        copy.start()
        pair_copies.append(copy)
    for copy in pair_copies:
        copy.wait_recv()

    lane_half = lax.broadcasted_iota(jnp.int32, (QUART, 128), 1) // TILE

    def picked(slot, d):
        tile = owner_ref[slot]
        near = table_ref[0, tile] + d
        far = table_ref[1, tile] + d
        z = g[near] + h[near]
        y = g[far] + h[far]
        return jnp.where(lane_half == table_ref[2, tile], z, pltpu.roll(y, TILE, 1))

    def ring_copy(d, step, s):
        src = buf.at[d, step, pl.ds(s * sub, sub)]
        dst = buf.at[d, step + 1, pl.ds(s * sub, sub)]
        target = device_of((pos + (1 if d == 0 else ring_n - 1)) % ring_n)
        return pltpu.make_async_remote_copy(
            src_ref=src, dst_ref=dst, send_sem=ring_send.at[d, step, s], recv_sem=ring_recv.at[d, step, s],
            device_id=target, device_id_type=MESH)

    def chunk_of(d, step):
        if d == 0:
            return (pos + 2 * ring_n - 1 - step) % ring_n
        return (pos + 1 + step) % ring_n

    base = [first_slot(chunk_of(d, 0)) for d in range(2)]

    @pl.loop(0, nsub)
    def _(s):
        for d in range(2):
            for k in range(sub):
                buf[d, 0, s * sub + k] = picked(base[d] + s * sub + k, d)
            ring_copy(d, 0, s).start()

    eye = (lax.broadcasted_iota(jnp.int32, (128, 128), 0) == lax.broadcasted_iota(jnp.int32, (128, 128), 1))
    for p in range(np_):
        block = tri(p) + p
        whole = (g[pl.ds(8 * block, 8)] + h[pl.ds(8 * block, 8)]).reshape(128, 128)
        both = jnp.where(eye, whole, 0.0)
        dg[pos, pl.ds(p, 1), :] = jnp.sum(both, axis=0, keepdims=True)

    def diag_copy(o):
        return pltpu.make_async_remote_copy(
            src_ref=dg.at[pos], dst_ref=dg.at[pos], send_sem=diag_send.at[o], recv_sem=diag_recv.at[o],
            device_id=device_of((pos + o) % ring_n), device_id_type=MESH)

    @pl.loop(1, ring_n)
    def _(o):
        diag_copy(o).start()

    def ring_step(step):
        first = [first_slot(chunk_of(d, step)) for d in range(2)]

        @pl.loop(0, nsub)
        def _(s):
            for d in range(2):
                ring_copy(d, step - 1, s).wait_recv()
                for k in range(sub):
                    buf[d, step, s * sub + k] += picked(first[d] + s * sub + k, d)
                ring_copy(d, step, s).start()

    split = min(3, ring_n - 1)

    @pl.loop(1, split)
    def _(step):
        ring_step(step)

    @pl.loop(1, ring_n)
    def _(o):
        diag_copy(o).wait_recv()

    total = dg[0]
    total = lax.fori_loop(1, ring_n, lambda r, acc: acc + dg[r], total)
    inverse = 1.0 / jnp.sqrt(total / features + 1e-06)
    for p in range(np_):
        line = inverse[p:p + 1, :]
        inv[p] = jnp.broadcast_to(line, (8, 128))
        across = jnp.broadcast_to(line, (128, 128)).T
        colb[2 * p] = across[:TILE]
        colb[2 * p + 1] = across[TILE:]

    own = (gx * gy_n + gy) * slots
    wide_half = lax.broadcasted_iota(jnp.int32, (HALF, 128), 1) // TILE
    one_half = lax.broadcasted_iota(jnp.int32, (8, 128), 1) // TILE
    root = 1.0 / jnp.sqrt(jnp.float32(features))

    @pl.loop(0, slots)
    def _(k):
        tile = owner_ref[own + k]
        down = colb[table_ref[3, tile]]
        down = jnp.where(wide_half == 0, down[:HALF], down[HALF:])
        line = inv[table_ref[4, tile]]
        line = jnp.where(one_half == table_ref[5, tile], line, pltpu.roll(line, TILE, 1))
        scale[k] = down * line[:1] * root

    @pl.loop(split, ring_n - 1)
    def _(step):
        ring_step(step)

    left = lax.broadcasted_iota(jnp.int32, (8, 128), 1) < TILE

    @pl.loop(0, nsub)
    def _(s):
        for d in range(2):
            ring_copy(d, ring_n - 2, s).wait_recv()
            for k in range(sub):
                n = s * sub + k
                value = buf[d, ring_n - 1, n] + picked(own + n, d)
                spot = (2 * k + d) * QUART
                pk[pl.ds(spot, QUART), :] = value * scale[n, d * QUART:(d + 1) * QUART, :]
                even = pk[pl.ds(spot, 8, stride=2), :]
                odd = pk[pl.ds(spot + 1, 8, stride=2), :]
                flat[pl.ds(pl.multiple_of(n * HALF + d * 8, 8), 8), :] = jnp.where(left, even, pltpu.roll(odd, TILE, 1))
                flat[pl.ds(pl.multiple_of(n * HALF + QUART + d * 8, 8), 8), :] = jnp.where(left, pltpu.roll(even, TILE, 1), odd)

    for r in range(HALF):
        out_ref[:, r * 128:(r + 1) * 128] = flat[pl.ds(r, slots, stride=HALF), :]

    for copy in pair_copies:
        copy.wait_send()

    @pl.loop(1, ring_n)
    def _(o):
        diag_copy(o).wait_send()

    @pl.loop(0, ring_n - 1)
    def _(step):
        @pl.loop(0, nsub)
        def _(s):
            for d in range(2):
                ring_copy(d, step, s).wait_send()


def shards(gx_n, gy_n, samples, tile_owner):
    ns, depth = samples.shape
    slots = tile_owner.shape[0] // (gx_n * gy_n)
    nsub = 4 if slots % 4 == 0 else 1
    ring_n = gx_n * gy_n // 2
    np_ = ns // 128
    blocks = 8 * tri(np_) + 4
    nload = -(-ns // ROWS)
    nlines = -(-np_ // 8) * 8
    cfg = (gx_n, gy_n, slots, nsub, depth * gx_n * gy_n)
    f32 = jnp.float32
    dma = pltpu.SemaphoreType.DMA
    table = jnp.asarray(tables(tile_owner.shape[0], ns // TILE))
    smem = pl.BlockSpec(memory_space=pltpu.SMEM)
    return pl.pallas_call(
        functools.partial(kernel, cfg),
        out_shape=jax.ShapeDtypeStruct((slots, TILE * TILE), f32),
        in_specs=[smem, smem, pl.BlockSpec(memory_space=pl.ANY)],
        out_specs=pl.BlockSpec(memory_space=pltpu.VMEM),
        scratch_shapes=[
            pltpu.VMEM((ns, depth), samples.dtype),
            pltpu.VMEM((blocks, QUART, 128), f32),
            pltpu.VMEM((blocks, QUART, 128), f32),
            pltpu.VMEM((2, ring_n, slots, QUART, 128), f32),
            pltpu.VMEM((ring_n, nlines, 128), f32),
            pltpu.VMEM((np_, 8, 128), f32),
            pltpu.VMEM((2 * np_, TILE, 128), f32),
            pltpu.VMEM((slots, HALF, 128), f32),
            pltpu.VMEM((2 * (slots // nsub) * QUART, 128), f32),
            pltpu.VMEM((slots * HALF, 128), f32),
            dma((nload,)), dma((nload,)), dma((nload,)),
            dma((ring_n,)), dma((ring_n,)),
            dma((2, ring_n - 1, nsub)), dma((2, ring_n - 1, nsub)),
        ],
        compiler_params=pltpu.CompilerParams(
            collective_id=0, has_side_effects=True, vmem_limit_bytes=56 * 1024 * 1024
        ),
    )(tile_owner, table, samples)


def solution(mesh):
    in_specs = (P("grp", ("gx", "gy")), P())
    out_specs = P(("grp", "gx", "gy"), None)
    body = functools.partial(shards, mesh.shape["gx"], mesh.shape["gy"])
    return jax.shard_map(body, mesh=mesh, in_specs=in_specs, out_specs=out_specs, check_vma=False)
```

```python
import functools

import jax
import jax.numpy as jnp
import numpy as np
from jax import lax
from jax.experimental import pallas as pl
from jax.experimental.pallas import tpu as pltpu
from jax.sharding import PartitionSpec as P

TILE = 64
HALF = TILE // 2
QUART = TILE // 4
ROWS = 512
MESH = pl.DeviceIdType.MESH


def tri(k):
    return k * (k + 1) // 2


def spots(ns):
    spot = {}
    for r0 in range(0, ns, ROWS):
        rows = range(r0 // 128, min(r0 + ROWS, ns) // 128)
        for c0 in range(0, r0 + 1, ROWS):
            for q in rows:
                for p in range(c0 // 128, min(q + 1, (c0 + ROWS) // 128)):
                    spot[q, p] = len(spot)
    return spot


def tables(slots_all, ns):
    spot = spots(ns)
    table = np.zeros((6, slots_all), np.int32)
    table[0], table[1] = 8 * len(spot), 8 * len(spot)
    t = 0
    for i in range(ns // TILE):
        for j in range(i + 1):
            first = 4 * (2 * spot[i // 2, j // 2] + i % 2)
            side = j % 2
            table[:, t] = (first + 2 * side, first + 2 * (1 - side), side, i, j // 2, side)
            t += 1
    assert t <= slots_all
    return table


def kernel(cfg, owner_ref, table_ref, x_ref, out_ref, a, g, h, buf, dg, inv, colb, scale, pk, flat,
           load_sem, pair_send, pair_recv, diag_send, diag_recv, ring_send, ring_recv):
    gx_n, gy_n, slots, nsub, features = cfg
    ring_n = gx_n * gy_n // 2
    sub = slots // nsub
    ns = a.shape[0]
    np_ = ns // 128
    gx, gy = lax.axis_index("gx"), lax.axis_index("gy")
    core = gy % 2
    row = gy // 2
    pos = row * gx_n + jnp.where(row % 2 == 0, gx, gx_n - 1 - gx)

    def coords_of(p):
        r = p // gx_n
        c = p % gx_n
        c = jnp.where(r % 2 == 0, c, gx_n - 1 - c)
        return c, r * 2 + core

    def device_of(p):
        c, y = coords_of(p)
        return {"gx": c, "gy": y}

    def first_slot(p):
        c, y = coords_of(p)
        return (c * gy_n + y) * slots

    partner = {"gx": gx, "gy": gy + 1 - 2 * core}

    starts = list(range(0, ns, ROWS))
    loads = []
    for n, r0 in enumerate(starts):
        size = min(ROWS, ns - r0)
        loads.append(pltpu.make_async_copy(x_ref.at[pl.ds(r0, size)], a.at[pl.ds(r0, size)], load_sem.at[n]))
        loads[-1].start()

    barrier = pltpu.get_barrier_semaphore()
    pl.semaphore_signal(barrier, inc=1, device_id=partner, device_id_type=MESH)

    @pl.loop(1, ring_n)
    def _(o):
        pl.semaphore_signal(barrier, inc=1, device_id=device_of((pos + o) % ring_n), device_id_type=MESH)

    dead = 8 * tri(np_)
    for n in range(4):
        g[dead + n] = jnp.zeros((QUART, 128), jnp.float32)
        h[dead + n] = jnp.zeros((QUART, 128), jnp.float32)

    def product(r0, size, c0, width):
        return lax.dot_general(
            a[pl.ds(r0, size), :], a[pl.ds(c0, width), :],
            (((1,), (1,)), ((), ())), preferred_element_type=jnp.float32,
        )

    def put(block, value):
        g[pl.ds(8 * block, 8)] = value.reshape(8, QUART, 128)

    spot = spots(ns)
    per = ROWS // 128
    pair_copies = []
    started = 0

    def pair_copy(first, last):
        many = pl.ds(8 * first, 8 * (last - first))
        n = len(pair_copies)
        pair_copies.append(pltpu.make_async_remote_copy(
            src_ref=g.at[many], dst_ref=h.at[many], send_sem=pair_send.at[n], recv_sem=pair_recv.at[n],
            device_id=partner, device_id_type=MESH))

    for n, r0 in enumerate(starts):
        size = min(ROWS, ns - r0)
        nq = size // 128
        q0 = r0 // 128
        loads[n].wait()

        if n:
            @pl.loop(0, n)
            def _(j):
                value = product(r0, size, pl.multiple_of(j * ROWS, ROWS), ROWS)
                for u in range(nq):
                    for v in range(per):
                        put(spot[q0, 0] + j * nq * per + u * per + v,
                            value[u * 128:(u + 1) * 128, v * 128:(v + 1) * 128])

            pair_copy(spot[q0, 0], spot[q0, q0])
            if not started:
                pl.semaphore_wait(barrier, ring_n)
            for copy in pair_copies[started:]:
                copy.start()
            started = len(pair_copies)

        value = product(r0, size, r0, size)
        for u in range(nq):
            for v in range(u + 1):
                put(spot[q0 + u, q0 + v], value[u * 128:(u + 1) * 128, v * 128:(v + 1) * 128])
        pair_copy(spot[q0, q0], spot[q0 + nq - 1, q0 + nq - 1] + 1)
        if started:
            pair_copies[-1].start()
            started += 1
    for copy in pair_copies:
        copy.wait_recv()

    lane_half = lax.broadcasted_iota(jnp.int32, (QUART, 128), 1) // TILE

    def picked(slot, d):
        tile = owner_ref[slot]
        near = table_ref[0, tile] + d
        far = table_ref[1, tile] + d
        z = g[near] + h[near]
        y = g[far] + h[far]
        return jnp.where(lane_half == table_ref[2, tile], z, pltpu.roll(y, TILE, 1))

    def ring_copy(d, step, s):
        src = buf.at[d, step, pl.ds(s * sub, sub)]
        dst = buf.at[d, step + 1, pl.ds(s * sub, sub)]
        target = device_of((pos + (1 if d == 0 else ring_n - 1)) % ring_n)
        return pltpu.make_async_remote_copy(
            src_ref=src, dst_ref=dst, send_sem=ring_send.at[d, step, s], recv_sem=ring_recv.at[d, step, s],
            device_id=target, device_id_type=MESH)

    def chunk_of(d, step):
        if d == 0:
            return (pos + 2 * ring_n - 1 - step) % ring_n
        return (pos + 1 + step) % ring_n

    base = [first_slot(chunk_of(d, 0)) for d in range(2)]

    @pl.loop(0, nsub)
    def _(s):
        for d in range(2):
            for k in range(sub):
                buf[d, 0, s * sub + k] = picked(base[d] + s * sub + k, d)
            ring_copy(d, 0, s).start()

    eye = (lax.broadcasted_iota(jnp.int32, (128, 128), 0) == lax.broadcasted_iota(jnp.int32, (128, 128), 1))
    for p in range(np_):
        block = spot[p, p]
        whole = (g[pl.ds(8 * block, 8)] + h[pl.ds(8 * block, 8)]).reshape(128, 128)
        both = jnp.where(eye, whole, 0.0)
        dg[pos, pl.ds(p, 1), :] = jnp.sum(both, axis=0, keepdims=True)

    def diag_copy(o):
        return pltpu.make_async_remote_copy(
            src_ref=dg.at[pos], dst_ref=dg.at[pos], send_sem=diag_send.at[o], recv_sem=diag_recv.at[o],
            device_id=device_of((pos + o) % ring_n), device_id_type=MESH)

    @pl.loop(1, ring_n)
    def _(o):
        diag_copy(o).start()

    def ring_step(step):
        first = [first_slot(chunk_of(d, step)) for d in range(2)]

        @pl.loop(0, nsub)
        def _(s):
            for d in range(2):
                ring_copy(d, step - 1, s).wait_recv()
                for k in range(sub):
                    buf[d, step, s * sub + k] += picked(first[d] + s * sub + k, d)
                ring_copy(d, step, s).start()

    split = min(3, ring_n - 1)

    @pl.loop(1, split)
    def _(step):
        ring_step(step)

    @pl.loop(1, ring_n)
    def _(o):
        diag_copy(o).wait_recv()

    total = dg[0]
    total = lax.fori_loop(1, ring_n, lambda r, acc: acc + dg[r], total)
    inverse = 1.0 / jnp.sqrt(total / features + 1e-06)
    for p in range(np_):
        line = inverse[p:p + 1, :]
        inv[p] = jnp.broadcast_to(line, (8, 128))
        across = jnp.broadcast_to(line, (128, 128)).T
        colb[2 * p] = across[:TILE]
        colb[2 * p + 1] = across[TILE:]

    own = (gx * gy_n + gy) * slots
    wide_half = lax.broadcasted_iota(jnp.int32, (HALF, 128), 1) // TILE
    one_half = lax.broadcasted_iota(jnp.int32, (8, 128), 1) // TILE
    root = 1.0 / jnp.sqrt(jnp.float32(features))

    @pl.loop(0, slots)
    def _(k):
        tile = owner_ref[own + k]
        down = colb[table_ref[3, tile]]
        down = jnp.where(wide_half == 0, down[:HALF], down[HALF:])
        line = inv[table_ref[4, tile]]
        line = jnp.where(one_half == table_ref[5, tile], line, pltpu.roll(line, TILE, 1))
        scale[k] = down * line[:1] * root

    @pl.loop(split, ring_n - 1)
    def _(step):
        ring_step(step)

    left = lax.broadcasted_iota(jnp.int32, (8, 128), 1) < TILE

    @pl.loop(0, nsub)
    def _(s):
        for d in range(2):
            ring_copy(d, ring_n - 2, s).wait_recv()
            for k in range(sub):
                n = s * sub + k
                value = buf[d, ring_n - 1, n] + picked(own + n, d)
                spot = (2 * k + d) * QUART
                pk[pl.ds(spot, QUART), :] = value * scale[n, d * QUART:(d + 1) * QUART, :]
                even = pk[pl.ds(spot, 8, stride=2), :]
                odd = pk[pl.ds(spot + 1, 8, stride=2), :]
                flat[pl.ds(pl.multiple_of(n * HALF + d * 8, 8), 8), :] = jnp.where(left, even, pltpu.roll(odd, TILE, 1))
                flat[pl.ds(pl.multiple_of(n * HALF + QUART + d * 8, 8), 8), :] = jnp.where(left, pltpu.roll(even, TILE, 1), odd)

    for r in range(HALF):
        out_ref[:, r * 128:(r + 1) * 128] = flat[pl.ds(r, slots, stride=HALF), :]

    for copy in pair_copies:
        copy.wait_send()

    @pl.loop(1, ring_n)
    def _(o):
        diag_copy(o).wait_send()

    @pl.loop(0, ring_n - 1)
    def _(step):
        @pl.loop(0, nsub)
        def _(s):
            for d in range(2):
                ring_copy(d, step, s).wait_send()


def shards(gx_n, gy_n, samples, tile_owner):
    ns, depth = samples.shape
    slots = tile_owner.shape[0] // (gx_n * gy_n)
    nsub = 4 if slots % 4 == 0 else 1
    ring_n = gx_n * gy_n // 2
    np_ = ns // 128
    blocks = 8 * tri(np_) + 4
    nload = -(-ns // ROWS)
    nlines = -(-np_ // 8) * 8
    cfg = (gx_n, gy_n, slots, nsub, depth * gx_n * gy_n)
    f32 = jnp.float32
    dma = pltpu.SemaphoreType.DMA
    table = jnp.asarray(tables(tile_owner.shape[0], ns))
    smem = pl.BlockSpec(memory_space=pltpu.SMEM)
    return pl.pallas_call(
        functools.partial(kernel, cfg),
        out_shape=jax.ShapeDtypeStruct((slots, TILE * TILE), f32),
        in_specs=[smem, smem, pl.BlockSpec(memory_space=pl.ANY)],
        out_specs=pl.BlockSpec(memory_space=pltpu.VMEM),
        scratch_shapes=[
            pltpu.VMEM((ns, depth), samples.dtype),
            pltpu.VMEM((blocks, QUART, 128), f32),
            pltpu.VMEM((blocks, QUART, 128), f32),
            pltpu.VMEM((2, ring_n, slots, QUART, 128), f32),
            pltpu.VMEM((ring_n, nlines, 128), f32),
            pltpu.VMEM((np_, 8, 128), f32),
            pltpu.VMEM((2 * np_, TILE, 128), f32),
            pltpu.VMEM((slots, HALF, 128), f32),
            pltpu.VMEM((2 * (slots // nsub) * QUART, 128), f32),
            pltpu.VMEM((slots * HALF, 128), f32),
            dma((nload,)), dma((2 * nload - 1,)), dma((2 * nload - 1,)),
            dma((ring_n,)), dma((ring_n,)),
            dma((2, ring_n - 1, nsub)), dma((2, ring_n - 1, nsub)),
        ],
        compiler_params=pltpu.CompilerParams(
            collective_id=0, has_side_effects=True, vmem_limit_bytes=56 * 1024 * 1024
        ),
    )(tile_owner, table, samples)


def solution(mesh):
    in_specs = (P("grp", ("gx", "gy")), P())
    out_specs = P(("grp", "gx", "gy"), None)
    body = functools.partial(shards, mesh.shape["gx"], mesh.shape["gy"])
    return jax.shard_map(body, mesh=mesh, in_specs=in_specs, out_specs=out_specs, check_vma=False)
```

```python
import functools

import jax
import jax.numpy as jnp
import numpy as np
from jax import lax
from jax.experimental import pallas as pl
from jax.experimental.pallas import tpu as pltpu
from jax.sharding import PartitionSpec as P

TILE = 64
HALF = TILE // 2
QUART = TILE // 4
ROWS = 512
MESH = pl.DeviceIdType.MESH


def tri(k):
    return k * (k + 1) // 2


def spots(ns):
    spot = {}
    for r0 in range(0, ns, ROWS):
        rows = range(r0 // 128, min(r0 + ROWS, ns) // 128)
        for c0 in range(0, r0 + 1, ROWS):
            for q in rows:
                for p in range(c0 // 128, min(q + 1, (c0 + ROWS) // 128)):
                    spot[q, p] = len(spot)
    return spot


def tables(slots_all, ns):
    spot = spots(ns)
    table = np.zeros((6, slots_all), np.int32)
    table[0], table[1] = 8 * len(spot), 8 * len(spot)
    t = 0
    for i in range(ns // TILE):
        for j in range(i + 1):
            first = 4 * (2 * spot[i // 2, j // 2] + i % 2)
            side = j % 2
            table[:, t] = (first + 2 * side, first + 2 * (1 - side), side, i, j // 2, side)
            t += 1
    assert t <= slots_all
    return table


def kernel(cfg, owner_ref, table_ref, x_ref, out_ref, a, g, h, buf, dg, inv, colb, scale, pk, flat,
           load_sem, pair_send, pair_recv, diag_send, diag_recv, ring_send, ring_recv):
    gx_n, gy_n, slots, nsub, features = cfg
    ring_n = gx_n * gy_n // 2
    sub = slots // nsub
    ns = a.shape[0]
    np_ = ns // 128
    gx, gy = lax.axis_index("gx"), lax.axis_index("gy")
    core = gy % 2
    row = gy // 2
    pos = row * gx_n + jnp.where(row % 2 == 0, gx, gx_n - 1 - gx)

    def coords_of(p):
        r = p // gx_n
        c = p % gx_n
        c = jnp.where(r % 2 == 0, c, gx_n - 1 - c)
        return c, r * 2 + core

    def device_of(p):
        c, y = coords_of(p)
        return {"gx": c, "gy": y}

    def first_slot(p):
        c, y = coords_of(p)
        return (c * gy_n + y) * slots

    partner = {"gx": gx, "gy": gy + 1 - 2 * core}

    starts = list(range(0, ns, ROWS))
    loads = []
    for n, r0 in enumerate(starts):
        size = min(ROWS, ns - r0)
        loads.append(pltpu.make_async_copy(x_ref.at[pl.ds(r0, size)], a.at[pl.ds(r0, size)], load_sem.at[n]))
        loads[-1].start()

    barrier = pltpu.get_barrier_semaphore()
    pl.semaphore_signal(barrier, inc=1, device_id=partner, device_id_type=MESH)

    @pl.loop(1, ring_n)
    def _(o):
        pl.semaphore_signal(barrier, inc=1, device_id=device_of((pos + o) % ring_n), device_id_type=MESH)

    dead = 8 * tri(np_)
    for n in range(4):
        g[dead + n] = jnp.zeros((QUART, 128), jnp.float32)
        h[dead + n] = jnp.zeros((QUART, 128), jnp.float32)

    def product(r0, size, c0, width):
        return lax.dot_general(
            a[pl.ds(r0, size), :], a[pl.ds(c0, width), :],
            (((1,), (1,)), ((), ())), preferred_element_type=jnp.float32,
        )

    def put(block, value):
        g[pl.ds(8 * block, 8)] = value.reshape(8, QUART, 128)

    spot = spots(ns)
    per = ROWS // 128
    pair_copies = []
    started = 0

    def pair_copy(first, last):
        many = pl.ds(8 * first, 8 * (last - first))
        n = len(pair_copies)
        pair_copies.append(pltpu.make_async_remote_copy(
            src_ref=g.at[many], dst_ref=h.at[many], send_sem=pair_send.at[n], recv_sem=pair_recv.at[n],
            device_id=partner, device_id_type=MESH))

    for n, r0 in enumerate(starts):
        size = min(ROWS, ns - r0)
        nq = size // 128
        q0 = r0 // 128
        loads[n].wait()

        if n:
            @pl.loop(0, n)
            def _(j):
                value = product(r0, size, pl.multiple_of(j * ROWS, ROWS), ROWS)
                for u in range(nq):
                    for v in range(per):
                        put(spot[q0, 0] + j * nq * per + u * per + v,
                            value[u * 128:(u + 1) * 128, v * 128:(v + 1) * 128])

            pair_copy(spot[q0, 0], spot[q0, q0])
            if not started:
                pl.semaphore_wait(barrier, ring_n)
            for copy in pair_copies[started:]:
                copy.start()
            started = len(pair_copies)

        value = product(r0, size, r0, size)
        for u in range(nq):
            for v in range(u + 1):
                put(spot[q0 + u, q0 + v], value[u * 128:(u + 1) * 128, v * 128:(v + 1) * 128])
        pair_copy(spot[q0, q0], spot[q0 + nq - 1, q0 + nq - 1] + 1)
        if started:
            pair_copies[-1].start()
            started += 1
    for copy in pair_copies:
        copy.wait_recv()

    lane_half = lax.broadcasted_iota(jnp.int32, (QUART, 128), 1) // TILE

    def picked(slot, d):
        tile = owner_ref[slot]
        near = table_ref[0, tile] + d
        far = table_ref[1, tile] + d
        z = g[near] + h[near]
        y = g[far] + h[far]
        return jnp.where(lane_half == table_ref[2, tile], z, pltpu.roll(y, TILE, 1))

    def ring_copy(d, step, s):
        src = buf.at[d, step, pl.ds(s * sub, sub)]
        dst = buf.at[d, step + 1, pl.ds(s * sub, sub)]
        target = device_of((pos + (1 if d == 0 else ring_n - 1)) % ring_n)
        return pltpu.make_async_remote_copy(
            src_ref=src, dst_ref=dst, send_sem=ring_send.at[d, step, s], recv_sem=ring_recv.at[d, step, s],
            device_id=target, device_id_type=MESH)

    def chunk_of(d, step):
        if d == 0:
            return (pos + 2 * ring_n - 1 - step) % ring_n
        return (pos + 1 + step) % ring_n

    base = [first_slot(chunk_of(d, 0)) for d in range(2)]

    @pl.loop(0, nsub)
    def _(s):
        for d in range(2):
            for k in range(sub):
                buf[d, 0, s * sub + k] = picked(base[d] + s * sub + k, d)
            ring_copy(d, 0, s).start()

    eye = (lax.broadcasted_iota(jnp.int32, (128, 128), 0) == lax.broadcasted_iota(jnp.int32, (128, 128), 1))
    for p in range(np_):
        block = spot[p, p]
        whole = (g[pl.ds(8 * block, 8)] + h[pl.ds(8 * block, 8)]).reshape(128, 128)
        both = jnp.where(eye, whole, 0.0)
        dg[pos, pl.ds(p, 1), :] = jnp.sum(both, axis=0, keepdims=True)

    def diag_copy(o):
        return pltpu.make_async_remote_copy(
            src_ref=dg.at[pos], dst_ref=dg.at[pos], send_sem=diag_send.at[o], recv_sem=diag_recv.at[o],
            device_id=device_of((pos + o) % ring_n), device_id_type=MESH)

    @pl.loop(1, ring_n)
    def _(o):
        diag_copy(o).start()

    def ring_step(step):
        first = [first_slot(chunk_of(d, step)) for d in range(2)]

        @pl.loop(0, nsub)
        def _(s):
            for d in range(2):
                ring_copy(d, step - 1, s).wait_recv()
                for k in range(sub):
                    buf[d, step, s * sub + k] += picked(first[d] + s * sub + k, d)
                ring_copy(d, step, s).start()

    split = min(3, ring_n - 1)

    @pl.loop(1, split)
    def _(step):
        ring_step(step)

    @pl.loop(1, ring_n)
    def _(o):
        diag_copy(o).wait_recv()

    total = dg[0]
    total = lax.fori_loop(1, ring_n, lambda r, acc: acc + dg[r], total)
    inverse = 1.0 / jnp.sqrt(total / features + 1e-06)
    for p in range(np_):
        line = inverse[p:p + 1, :]
        inv[p] = jnp.broadcast_to(line, (8, 128))
        across = jnp.broadcast_to(line, (128, 128)).T
        colb[2 * p] = across[:TILE]
        colb[2 * p + 1] = across[TILE:]

    own = (gx * gy_n + gy) * slots
    wide_half = lax.broadcasted_iota(jnp.int32, (HALF, 128), 1) // TILE
    one_half = lax.broadcasted_iota(jnp.int32, (8, 128), 1) // TILE
    root = 1.0 / jnp.sqrt(jnp.float32(features))

    @pl.loop(0, slots)
    def _(k):
        tile = owner_ref[own + k]
        down = colb[table_ref[3, tile]]
        down = jnp.where(wide_half == 0, down[:HALF], down[HALF:])
        line = inv[table_ref[4, tile]]
        line = jnp.where(one_half == table_ref[5, tile], line, pltpu.roll(line, TILE, 1))
        scale[k] = down * line[:1] * root

    @pl.loop(split, ring_n - 1)
    def _(step):
        ring_step(step)

    left = lax.broadcasted_iota(jnp.int32, (8, 128), 1) < TILE

    @pl.loop(0, nsub)
    def _(s):
        for d in range(2):
            ring_copy(d, ring_n - 2, s).wait_recv()
            for k in range(sub):
                n = s * sub + k
                value = buf[d, ring_n - 1, n] + picked(own + n, d)
                spot = (2 * k + d) * QUART
                pk[pl.ds(spot, QUART), :] = value * scale[n, d * QUART:(d + 1) * QUART, :]
                even = pk[pl.ds(spot, 8, stride=2), :]
                odd = pk[pl.ds(spot + 1, 8, stride=2), :]
                flat[pl.ds(pl.multiple_of(n * HALF + d * 8, 8), 8), :] = jnp.where(left, even, pltpu.roll(odd, TILE, 1))
                flat[pl.ds(pl.multiple_of(n * HALF + QUART + d * 8, 8), 8), :] = jnp.where(left, pltpu.roll(even, TILE, 1), odd)

    for r in range(HALF):
        out_ref[:, r * 128:(r + 1) * 128] = flat[pl.ds(r, slots, stride=HALF), :]

    for copy in pair_copies:
        copy.wait_send()

    @pl.loop(1, ring_n)
    def _(o):
        diag_copy(o).wait_send()

    @pl.loop(0, ring_n - 1)
    def _(step):
        @pl.loop(0, nsub)
        def _(s):
            for d in range(2):
                ring_copy(d, step, s).wait_send()


def shards(gx_n, gy_n, samples, tile_owner):
    ns, depth = samples.shape
    slots = tile_owner.shape[0] // (gx_n * gy_n)
    nsub = 4 if slots % 4 == 0 else 1
    ring_n = gx_n * gy_n // 2
    np_ = ns // 128
    blocks = 8 * tri(np_) + 4
    nload = -(-ns // ROWS)
    cfg = (gx_n, gy_n, slots, nsub, depth * gx_n * gy_n)
    f32 = jnp.float32
    dma = pltpu.SemaphoreType.DMA
    table = jnp.asarray(tables(tile_owner.shape[0], ns))
    smem = pl.BlockSpec(memory_space=pltpu.SMEM)
    return pl.pallas_call(
        functools.partial(kernel, cfg),
        out_shape=jax.ShapeDtypeStruct((slots, TILE * TILE), f32),
        in_specs=[smem, smem, pl.BlockSpec(memory_space=pl.ANY)],
        out_specs=pl.BlockSpec(memory_space=pltpu.VMEM),
        scratch_shapes=[
            pltpu.VMEM((ns, depth), samples.dtype),
            pltpu.VMEM((blocks, QUART, 128), f32),
            pltpu.VMEM((blocks, QUART, 128), f32),
            pltpu.VMEM((2, ring_n, slots, QUART, 128), f32),
            pltpu.VMEM((ring_n, np_, 128), f32),
            pltpu.VMEM((np_, 8, 128), f32),
            pltpu.VMEM((2 * np_, TILE, 128), f32),
            pltpu.VMEM((slots, HALF, 128), f32),
            pltpu.VMEM((2 * (slots // nsub) * QUART + 8, 128), f32),
            pltpu.VMEM(((slots + 1) * HALF, 128), f32),
            dma((nload,)), dma((2 * nload - 1,)), dma((2 * nload - 1,)),
            dma((ring_n,)), dma((ring_n,)),
            dma((2, ring_n - 1, nsub)), dma((2, ring_n - 1, nsub)),
        ],
        compiler_params=pltpu.CompilerParams(
            collective_id=0, has_side_effects=True, vmem_limit_bytes=56 * 1024 * 1024
        ),
    )(tile_owner, table, samples)


def solution(mesh):
    in_specs = (P("grp", ("gx", "gy")), P())
    out_specs = P(("grp", "gx", "gy"), None)
    body = functools.partial(shards, mesh.shape["gx"], mesh.shape["gy"])
    return jax.shard_map(body, mesh=mesh, in_specs=in_specs, out_specs=out_specs, check_vma=False)
```
